32 devices in a mesh: groups: 2 (over x), space: 16 (over z, y, core).
Axes of the slice: x: 2, y: 2, z: 4, core: 2. Of those that a mesh axis runs over, the one named last changes fastest.
Arguments:
- noisy: bfloat16 [16384, 512], P(('groups', 'space')), parts along dimension 0, may hold values from -6 to 6
- matches: int32 [3072, 16], P(('groups', 'space')), parts along dimension 0, may hold values from 0 to 8191, as said below
- cube_home: int32 [16384], P('groups'), parts along dimension 0, may hold values from 0 to 8191, as said below
- sigma_coef: float32 [512], replicated, may hold values from 0.3 to 1.5
Outputs:
- basic: bfloat16 [16384, 512], P(('groups', 'space')), parts along dimension 0
- final: bfloat16 [16384, 512], P(('groups', 'space')), parts along dimension 0
The draws below stay inside these ranges and needn't reach their ends.
There are 2 independent parts, one for each index of `groups`. The reference program is written for one: setup_inputs(seed, part) draws one part's arguments, and reference() takes and returns one part's arrays. A program takes and returns all parts, laid end to end along the dimension named above; an argument that names none is the same for every part. Nothing has to cross between parts.
Inputs may be any that keep to these rules, and one draw needn't show every extreme that they name: `matches`: each device's 16 * 96 list entries name at most 192 cubes whose table rows lie in any one device's block of 512 rows; in every draw one block receives exactly 192 from every device. `cube_home`: A permutation of the table rows.
All inputs are finite; a program needn't handle non-finite values.
Results may differ from the reference program's by a relative error of at most 0.0079.
Values may be sent and summed in bfloat16 or wider, within the bound.
A program may use at most 64 MiB of HBM per device.

```python
import math
import jax
import jax.numpy as jnp
from jax import lax

CUBE = 512
M = 16
REF_DEV = 96
CUBES_DEV = 512
CUBES = 8192
CAP = 192
N_SPACE = 16


def make_plan(key):
    base = jax.random.fold_in(key, 7)
    key_home, key_hot, key_slots, key_mix, key_local = jax.random.split(base, 5)
    entries = M * REF_DEV
    places = N_SPACE * CAP
    home = jax.random.permutation(key_home, CUBES_DEV * N_SPACE)
    hotter = jax.random.randint(key_hot, (), 0, N_SPACE)
    slot_keys = jax.random.split(key_slots, N_SPACE)
    orders = jax.vmap(lambda k: jax.random.permutation(k, places))(slot_keys)
    holder = jnp.arange(places, dtype=jnp.int32) // CAP
    scores = orders + jnp.where(holder == hotter, 0, places)[None, :]
    chosen = jnp.argsort(scores, axis=1, stable=True)[:, :entries]
    mix_keys = jax.random.split(key_mix, N_SPACE)
    mixing = jax.vmap(lambda k: jax.random.permutation(k, entries))(mix_keys)
    chosen = jnp.take_along_axis(chosen, mixing, axis=1)
    owner = chosen // CAP
    local = jax.random.randint(key_local, (N_SPACE, entries), 0, CUBES_DEV)
    table_row = owner * CUBES_DEV + local
    identity = jnp.argsort(home, stable=True).astype(jnp.int32)
    ids = identity[table_row.reshape(-1)].reshape(N_SPACE * REF_DEV, M)
    return (home.astype(jnp.int32), ids.astype(jnp.int32))


def draw_cube_home(key, part):
    return make_plan(key)[0]


def draw_matches(key, part):
    return make_plan(key)[1]


def level_of(own_key, extent, shards, smallest, high):
    def one(position, blocks):
        heights = jax.random.uniform(jax.random.fold_in(jax.random.fold_in(own_key, 6), position), (blocks,), jnp.float32, smallest / len(shards), high / len(shards))
        return jnp.repeat(jnp.exp(heights), extent[position] // blocks).reshape((-1,) + (1,) * (len(extent) - position - 1))

    loudness = one(*shards[0])
    for cut in shards[1:]:
        loudness = loudness * one(*cut)
    return loudness


def gaussian(rng, dims, deviation, reach, cuts=(), kind=jnp.bfloat16):
    drawn = deviation * jax.random.normal(rng, dims, jnp.float32)
    if cuts:
        drawn = drawn * level_of(rng, dims, cuts, -0.22, 0.18)
    return jnp.clip(drawn, -reach, reach).astype(kind)


def setup_inputs(seed: int = 0, part: int = 0) -> dict:
    arg_keys = jax.random.split(jax.random.key(seed), 5)
    own_keys = jax.random.split(jax.random.fold_in(arg_keys[4], part), 5)
    return {
        "noisy": gaussian(own_keys[0], (CUBES, CUBE), 1.0, 6.0, ((0, 16),)),
        "matches": draw_matches(jax.random.fold_in(jax.random.fold_in(arg_keys[4], part), 71), part),
        "cube_home": draw_cube_home(jax.random.fold_in(jax.random.fold_in(arg_keys[4], part), 71), part),
        "sigma_coef": jnp.clip(jnp.exp(jax.random.uniform(arg_keys[3], (CUBE,), jnp.float32, math.log(0.3), math.log(1.5))), 0.3, 1.5),
    }


shrink_level = 2.7
prior_weight = 0.5

def dct_matrix(length):
    index = jnp.arange(length, dtype=jnp.float32)
    freq = index[:, None]
    table = jnp.cos(jnp.pi * (2.0 * index[None, :] + 1.0) * freq / (2.0 * length)) * jnp.sqrt(2.0 / length)
    return jnp.where(freq == 0, table / jnp.sqrt(2.0), table)

def make_tables(group):
    small = dct_matrix(8)
    cube_table = jnp.einsum('ad,be,cf->abcdef', small, small, small).reshape(512, 512).astype(jnp.bfloat16)
    return (cube_table, dct_matrix(group))

def forward(members, cube_table, group_table):
    spec = jnp.dot(members.reshape(-1, members.shape[-1]), cube_table.T, preferred_element_type=jnp.float32)
    spec = spec.reshape(members.shape)
    return jnp.einsum('jm,rmk->rjk', group_table, spec, precision=lax.Precision.HIGHEST)

def backward(coeffs, cube_table, group_table):
    back = jnp.einsum('jm,rjk->rmk', group_table, coeffs, precision=lax.Precision.HIGHEST).astype(jnp.bfloat16)
    out = jnp.dot(back.reshape(-1, back.shape[-1]), cube_table, preferred_element_type=jnp.float32)
    return out.reshape(coeffs.shape)

def aggregate(parts, weights, targets, noisy, count):
    numer = jax.ops.segment_sum(parts.astype(jnp.float32), targets, count)
    denom = jax.ops.segment_sum(weights.astype(jnp.float32), targets, count)
    return ((numer + prior_weight * noisy.astype(jnp.float32)) / (denom[:, None] + prior_weight)).astype(jnp.bfloat16)

def first_phase(coeffs, sigma_coef, cube_table, group_table):
    level = (shrink_level * sigma_coef) ** 2
    square = coeffs * coeffs
    gain = square / (square + level)
    weight = 1.0 / (0.25 + lax.optimization_barrier(jnp.mean(gain * gain, axis=(1, 2))))
    out = backward(gain * coeffs, cube_table, group_table)
    part = (weight[:, None, None] * out).astype(jnp.bfloat16)
    wcopy = jnp.broadcast_to(weight[:, None], out.shape[:2]).astype(jnp.bfloat16)
    return (part, wcopy)

def second_phase(coeffs, gcoeffs, sigma_coef, cube_table, group_table):
    noise = sigma_coef * sigma_coef
    square = gcoeffs * gcoeffs
    wiener = square / (square + noise)
    weight = 1.0 / (0.25 + lax.optimization_barrier(jnp.mean(wiener * wiener * noise, axis=(1, 2))))
    out = backward(wiener * coeffs, cube_table, group_table)
    part = (weight[:, None, None] * out).astype(jnp.bfloat16)
    wcopy = jnp.broadcast_to(weight[:, None], out.shape[:2]).astype(jnp.bfloat16)
    return (part, wcopy)

def reference(noisy, matches, cube_home, sigma_coef):
    cube_table, group_table = make_tables(matches.shape[1])
    rows = cube_home[matches]
    flat_rows = rows.reshape(-1)
    count = noisy.shape[0]
    width = noisy.shape[1]
    members = noisy[rows]
    coeffs = forward(members, cube_table, group_table)
    part, wcopy = first_phase(coeffs, sigma_coef, cube_table, group_table)
    basic = aggregate(part.reshape(-1, width), wcopy.reshape(-1), flat_rows, noisy, count)
    guide = basic[rows]
    gcoeffs = forward(guide, cube_table, group_table)
    part2, wcopy2 = second_phase(coeffs, gcoeffs, sigma_coef, cube_table, group_table)
    final = aggregate(part2.reshape(-1, width), wcopy2.reshape(-1), flat_rows, noisy, count)
    return (basic, final)
```

```python
import functools

import jax
import jax.numpy as jnp
import numpy as np
from jax import lax
from jax.experimental import pallas as pl
from jax.experimental.pallas import tpu as pltpu
from jax.sharding import PartitionSpec as P

shrink_level = 2.7
prior_weight = 0.5
LANES = 128
CHUNK = 512
ROWS = 256


def dct_matrix(length):
    index = np.arange(length, dtype=np.float64)
    table = np.cos(np.pi * (2.0 * index[None, :] + 1.0) * index[:, None] / (2.0 * length))
    table = table * np.sqrt(2.0 / length)
    table[0] /= np.sqrt(2.0)
    return table


def make_tables(group):
    small = dct_matrix(8)
    cube = np.kron(np.kron(small, small), small).astype(np.float32)
    mix = np.kron(np.eye(LANES // group), dct_matrix(group)).astype(np.float32)
    return jnp.asarray(cube, jnp.bfloat16), jnp.asarray(cube.T, jnp.bfloat16), mix, mix.T.copy()


def mix_rows(table, value):
    pieces = [
        jnp.dot(
            table,
            value[i : i + LANES],
            precision=lax.Precision.HIGHEST,
            preferred_element_type=jnp.float32,
        )
        for i in range(0, value.shape[0], LANES)
    ]
    return jnp.concatenate(pieces, axis=0)


def kernel(second, group, *refs):
    if second:
        (home, ids, sigma, cube, cube_t, mix, mix_t, coeffs, table, acc_out, wsum) = refs[:11]
        big, members, wacc, wref, stage, sem = refs[11:]
    else:
        (home, ids, sigma, cube, cube_t, mix, mix_t, table, coeffs, acc_out, wsum) = refs[:11]
        big, members, wacc, wref, stage, sem = refs[11:]
    cubes, width = table.shape
    entries = members.shape[0]
    chunks = cubes // CHUNK

    def fetch(i, slot):
        rows = pl.ds(pl.multiple_of(i * CHUNK, CHUNK), CHUNK)
        return pltpu.make_async_copy(table.at[rows, :], stage.at[slot], sem.at[slot])

    fetch(0, 0).start()

    def load_step(i, carry):
        slot = lax.rem(i, 2)

        @pl.when(i + 1 < chunks)
        def _():
            fetch(i + 1, 1 - slot).start()

        fetch(i, slot).wait()
        rows = pl.ds(pl.multiple_of(i * CHUNK, CHUNK), CHUNK)
        big[rows, :] = stage[slot].astype(jnp.float32)
        return carry

    lax.fori_loop(0, chunks, load_step, 0)

    def gather_step(r, carry):
        base = pl.multiple_of(r * group, group)
        picked = [big[pl.ds(home[ids[base + m]], 1), :] for m in range(group)]
        for m in range(group):
            members[pl.ds(base + m, 1), :] = picked[m]
        return carry

    lax.fori_loop(0, entries // group, gather_step, 0)

    noise = sigma[...] * sigma[...]
    level = (shrink_level * sigma[...]) * (shrink_level * sigma[...])

    def compute_step(b, carry):
        rows = pl.ds(pl.multiple_of(b * ROWS, ROWS), ROWS)
        spec = jnp.dot(
            members[rows, :].astype(jnp.bfloat16), cube_t[...], preferred_element_type=jnp.float32
        )
        own = mix_rows(mix[...], spec)
        square = own * own
        if second:
            gain = square / (square + noise)
            energy = gain * gain * noise
            shrunk = gain * coeffs[rows, :]
        else:
            coeffs[rows, :] = own
            gain = square / (square + level)
            energy = gain * gain
            shrunk = gain * own
        refs_here = ROWS // group
        total = jnp.sum(jnp.sum(energy, axis=1, keepdims=True).reshape(refs_here, group, 1), axis=1)
        weight = 1.0 / (0.25 + total / (group * width))
        back = mix_rows(mix_t[...], shrunk).astype(jnp.bfloat16)
        out = jnp.dot(back, cube[...], preferred_element_type=jnp.float32)
        each = jnp.broadcast_to(weight[:, None, :], (refs_here, group, 1)).reshape(ROWS, 1)
        members[rows, :] = (each * out).astype(jnp.bfloat16).astype(jnp.float32)
        wref[pl.ds(pl.multiple_of(b * refs_here, refs_here), refs_here), :] = jnp.broadcast_to(
            weight.astype(jnp.bfloat16).astype(jnp.float32), (refs_here, LANES)
        )
        return carry

    lax.fori_loop(0, entries // ROWS, compute_step, 0)

    def zero_step(i, carry):
        rows = pl.ds(pl.multiple_of(i * CHUNK, CHUNK), CHUNK)
        big[rows, :] = jnp.zeros((CHUNK, width), jnp.float32)
        wacc[rows, :] = jnp.zeros((CHUNK, LANES), jnp.float32)
        return carry

    lax.fori_loop(0, chunks, zero_step, 0)

    def scatter_step(r, carry):
        base = pl.multiple_of(r * group, group)
        wrow = wref[pl.ds(r, 1), :]
        for m in range(group):
            row = pl.ds(home[ids[base + m]], 1)
            big[row, :] += members[pl.ds(base + m, 1), :]
            wacc[row, :] += wrow
        return carry

    lax.fori_loop(0, entries // group, scatter_step, 0)

    def put(i, slot):
        rows = pl.ds(pl.multiple_of(i * CHUNK, CHUNK), CHUNK)
        return pltpu.make_async_copy(stage.at[slot], acc_out.at[rows, :], sem.at[slot])

    def store_step(i, carry):
        slot = lax.rem(i, 2)

        @pl.when(i >= 2)
        def _():
            put(i - 2, slot).wait()

        rows = pl.ds(pl.multiple_of(i * CHUNK, CHUNK), CHUNK)
        stage[slot] = big[rows, :].astype(jnp.bfloat16)
        put(i, slot).start()
        return carry

    lax.fori_loop(0, chunks, store_step, 0)

    lane = lax.broadcasted_iota(jnp.int32, (LANES, LANES), 1)
    sub = lax.broadcasted_iota(jnp.int32, (LANES, LANES), 0)

    def weight_step(i, carry):
        rows = pl.ds(pl.multiple_of(i * LANES, LANES), LANES)
        wsum[pl.ds(i, 1), :] = jnp.sum(
            jnp.where(lane == sub, wacc[rows, :], 0.0), axis=0, keepdims=True
        )
        return carry

    lax.fori_loop(0, cubes // LANES, weight_step, 0)
    for i in (chunks - 2, chunks - 1):
        put(i, i % 2).wait()


def phase(second, home, ids, sigma, tables, table, group, coeffs=None):
    cubes, width = table.shape
    entries = ids.shape[0]
    vmem = pl.BlockSpec(memory_space=pltpu.VMEM)
    smem = pl.BlockSpec(memory_space=pltpu.SMEM)
    anywhere = pl.BlockSpec(memory_space=pltpu.HBM)
    held = jax.ShapeDtypeStruct((entries, width), jnp.float32)
    outs = [
        jax.ShapeDtypeStruct((cubes, width), jnp.bfloat16),
        jax.ShapeDtypeStruct((cubes // LANES, LANES), jnp.float32),
    ]
    out_specs = [anywhere, vmem]
    in_specs = [smem, smem] + [vmem] * 5
    args = [home, ids, sigma, *tables]
    if second:
        in_specs = in_specs + [vmem, anywhere]
        args = args + [coeffs, table]
    else:
        in_specs = in_specs + [anywhere]
        args = args + [table]
        outs = [held] + outs
        out_specs = [vmem] + out_specs
    return pl.pallas_call(
        functools.partial(kernel, second, group),
        out_shape=outs,
        in_specs=in_specs,
        out_specs=out_specs,
        scratch_shapes=[
            pltpu.VMEM((cubes, width), jnp.float32),
            pltpu.VMEM((entries, width), jnp.float32),
            pltpu.VMEM((cubes, LANES), jnp.float32),
            pltpu.VMEM((entries // group, LANES), jnp.float32),
            pltpu.VMEM((2, CHUNK, width), jnp.bfloat16),
            pltpu.SemaphoreType.DMA((2,)),
        ],
        compiler_params=pltpu.CompilerParams(vmem_limit_bytes=60 * 1024 * 1024),
        name="wiener" if second else "shrink",
    )(*args)


MESH = pl.DeviceIdType.MESH


class Ring:
    def __init__(self, grid, count):
        self.grid, self.chips = grid, count // 2
        self.me = lax.axis_index("space")
        self.core = lax.rem(self.me, 2)
        self.spot = self.spot_of(self.me // 2)
        self.partner = {"space": self.me + 1 - 2 * self.core}
        self.sides = tuple({"space": self.device(sign, self.core)} for sign in (1, -1))

    def spot_of(self, chip):
        if self.grid == 1:
            return chip
        side, along = lax.rem(chip, 2), chip // 2
        return along + side * (self.chips - 1 - 2 * along)

    def chip(self, offset):
        spot = lax.rem(self.spot + offset + self.chips, self.chips)
        if self.grid == 1:
            return spot
        side = (2 * spot) // self.chips
        return (spot + side * (self.chips - 1 - 2 * spot)) * 2 + side

    def device(self, offset, core):
        return self.chip(offset) * 2 + core

    def greet(self):
        barrier = pltpu.get_barrier_semaphore()
        for device in (*self.sides, self.partner):
            pl.semaphore_signal(barrier, inc=1, device_id=device, device_id_type=MESH)
        pl.semaphore_wait(barrier, 3)


def hops(chips, pieces):
    far = chips // 2
    orders = []
    for way in range(2):
        halves = range(pieces // 2) if way == 0 else range(pieces // 2, pieces)
        orders.append([(d, j) for d in range(1, far) for j in range(pieces)] + [(far, j) for j in halves])
    return orders


def remote(src, dst, send, recv, device):
    return pltpu.make_async_remote_copy(
        src_ref=src, dst_ref=dst, send_sem=send, recv_sem=recv, device_id=device, device_id_type=MESH
    )


def gather_kernel(grid, x, out, send, recv, give, take, own):
    count, held = out.shape[:2]
    pieces = held // LANES
    ring = Ring(grid, count)
    orders = hops(ring.chips, pieces)
    where = [{key: t for t, key in enumerate(order)} for order in orders]
    last = len(orders[0])
    ring.greet()

    def part(block, j):
        return out.at[block, pl.ds(j * LANES, LANES), :]

    started = []

    def start(copy):
        copy.start()
        started.append(copy)

    for j in range(pieces):
        for way in range(2):
            if (1, j) in where[way]:
                t = where[way][(1, j)]
                start(
                    remote(
                        x.at[pl.ds(j * LANES, LANES), :],
                        part(ring.me, j),
                        send.at[way, t],
                        recv.at[way, t],
                        ring.sides[way],
                    )
                )
    keep = pltpu.make_async_copy(x, out.at[ring.me], own.at[0])
    keep.start()
    start(remote(x, out.at[ring.me], give.at[0, last], take.at[0, last], ring.partner))
    for t in range(last):
        for way in range(2):
            d, j = orders[way][t]
            block = ring.device(-d if way == 0 else d, ring.core)
            piece = part(block, j)
            remote(piece, piece, send.at[way, t], recv.at[way, t], ring.sides[way]).wait_recv()
            onward = where[way].get((d + 1, j))
            if onward is not None:
                start(
                    remote(
                        piece, piece, send.at[way, onward], recv.at[way, onward], ring.sides[way]
                    )
                )
            start(remote(piece, piece, give.at[way, t], take.at[way, t], ring.partner))
    other = ring.me + 1 - 2 * ring.core
    remote(
        out.at[other], out.at[other], give.at[0, last], take.at[0, last], ring.partner
    ).wait_recv()
    for t in range(last):
        for way in range(2):
            d, j = orders[way][t]
            piece = part(ring.device(-d if way == 0 else d, 1 - ring.core), j)
            remote(piece, piece, give.at[way, t], take.at[way, t], ring.partner).wait_recv()
    for copy in started:
        copy.wait_send()
    keep.wait()


def gather_all(x, grid):
    count = lax.axis_size("space")
    held, width = x.shape
    last = len(hops(count // 2, held // LANES)[0])
    sems = pltpu.SemaphoreType.DMA
    out = pl.pallas_call(
        functools.partial(gather_kernel, grid),
        out_shape=jax.ShapeDtypeStruct((count, held, width), x.dtype),
        in_specs=[pl.BlockSpec(memory_space=pltpu.VMEM)],
        out_specs=pl.BlockSpec(memory_space=pltpu.HBM),
        scratch_shapes=[
            sems((2, last)),
            sems((2, last)),
            sems((2, last + 1)),
            sems((2, last + 1)),
            sems((1,)),
        ],
        compiler_params=pltpu.CompilerParams(collective_id=0, has_side_effects=True),
        name="spread",
    )(x)
    return out.reshape(count * held, width)


def reduce_kernel(grid, acc, wsum, noisy, out, own, other, got, sent, wother, wgot, wsent, *sems):
    own_sem, give, take, send, recv, wgive, wtake, wsend, wrecv = sems
    chips = acc.shape[0]
    pieces = acc.shape[2] // LANES
    ring = Ring(grid, 2 * chips)
    far = chips // 2
    orders = [
        sorted(order, key=lambda key: (-key[0], key[1])) for order in hops(chips, pieces)
    ]
    where = [{key: t for t, key in enumerate(order)} for order in orders]
    last = len(orders[0])
    offsets = [far] + [s * d for d in range(far - 1, 0, -1) for s in (1, -1)] + [0]
    slot_of = {off: i for i, off in enumerate(offsets)}
    slot_of[-far] = 0
    started, local, gifts = [], [], []

    for i, off in enumerate(offsets):
        copy = pltpu.make_async_copy(acc.at[ring.chip(off), ring.core], own.at[i], own_sem.at[i])
        copy.start()
        local.append(copy)
    ring.greet()
    for i, off in enumerate(offsets):
        copy = remote(
            acc.at[ring.chip(off), 1 - ring.core], other.at[i], give.at[i], take.at[i], ring.partner
        )
        copy.start()
        gifts.append(copy)
        if i == 0:
            wgift = remote(wsum, wother, wgive.at[0], wtake.at[0], ring.partner)
            wgift.start()
    ready = set()

    def settle_slot(i):
        if i not in ready:
            ready.add(i)
            local[i].wait()
            gifts[i].wait_recv()

    def value(off, j, ways, d):
        i = slot_of[off]
        settle_slot(i)
        rows = pl.ds(j * LANES, LANES)
        total = own[i, rows, :].astype(jnp.float32) + other[i, rows, :].astype(jnp.float32)
        for way in ways:
            t = where[way].get((d + 1, j))
            if t is not None:
                piece = got.at[way, t]
                remote(sent.at[way, t], piece, send.at[way, t], recv.at[way, t], ring.sides[way]).wait_recv()
                total = total + piece[...].astype(jnp.float32)
        return total

    def weights(off, ways, d):
        chip = ring.chip(off)
        if "w" not in ready:
            ready.add("w")
            wgift.wait_recv()
        total = wsum[chip, ring.core] + wother[chip, ring.core]
        for way in ways:
            if d + 1 < far or (d + 1 == far and way == 0):
                remote(
                    wsent.at[way, d + 1],
                    wgot.at[way, d + 1],
                    wsend.at[way, d + 1],
                    wrecv.at[way, d + 1],
                    ring.sides[way],
                ).wait_recv()
                total = total + wgot[way, d + 1]
        return total

    for t in range(last):
        for way in range(2):
            d, j = orders[way][t]
            off = d if way == 0 else -d
            sent[way, t] = value(off, j, (way,), d).astype(sent.dtype)
            copy = remote(sent.at[way, t], got.at[way, t], send.at[way, t], recv.at[way, t], ring.sides[way])
            copy.start()
            started.append(copy)
            final_piece = t + 1 == last or orders[way][t + 1][0] != d
            if final_piece and (d < far or way == 0):
                wsent[way, d] = weights(off, (way,), d)
                copy = remote(
                    wsent.at[way, d], wgot.at[way, d], wsend.at[way, d], wrecv.at[way, d], ring.sides[way]
                )
                copy.start()
                started.append(copy)
    lane = lax.broadcasted_iota(jnp.int32, (LANES, LANES), 1)
    sub = lax.broadcasted_iota(jnp.int32, (LANES, LANES), 0)
    denom = weights(0, (0, 1), 0)
    for j in range(pieces):
        rows = pl.ds(j * LANES, LANES)
        numer = value(0, j, (0, 1), 0) + prior_weight * noisy[rows, :].astype(jnp.float32)
        spread = jnp.broadcast_to(denom[j : j + 1, :], (LANES, LANES))
        column = jnp.sum(jnp.where(lane == sub, spread, 0.0), axis=1, keepdims=True)
        out[rows, :] = (numer / (column + prior_weight)).astype(out.dtype)
    for copy in started + gifts + [wgift]:
        copy.wait_send()


def settle(acc, wsum, noisy, grid):
    count = lax.axis_size("space")
    held, width = noisy.shape
    chips, pieces = count // 2, held // LANES
    far = chips // 2
    last = len(hops(chips, pieces)[0])
    sems = pltpu.SemaphoreType.DMA
    vmem = pl.BlockSpec(memory_space=pltpu.VMEM)
    small = (chips, 2, pieces, LANES)
    return pl.pallas_call(
        functools.partial(reduce_kernel, grid),
        out_shape=jax.ShapeDtypeStruct(noisy.shape, noisy.dtype),
        in_specs=[pl.BlockSpec(memory_space=pltpu.HBM), vmem, vmem],
        out_specs=vmem,
        scratch_shapes=[
            pltpu.VMEM((chips, held, width), acc.dtype),
            pltpu.VMEM((chips, held, width), acc.dtype),
            pltpu.VMEM((2, last, LANES, width), acc.dtype),
            pltpu.VMEM((2, last, LANES, width), acc.dtype),
            pltpu.VMEM(small, jnp.float32),
            pltpu.VMEM((2, far + 1, pieces, LANES), jnp.float32),
            pltpu.VMEM((2, far + 1, pieces, LANES), jnp.float32),
            sems((chips,)),
            sems((chips,)),
            sems((chips,)),
            sems((2, last)),
            sems((2, last)),
            sems((1,)),
            sems((1,)),
            sems((2, far + 1)),
            sems((2, far + 1)),
        ],
        compiler_params=pltpu.CompilerParams(
            collective_id=1, has_side_effects=True, vmem_limit_bytes=60 * 1024 * 1024
        ),
        name="settle",
    )(acc.reshape(chips, 2, held, width), wsum.reshape(small), noisy)


def body(grid, noisy, matches, cube_home, sigma_coef):
    group = matches.shape[1]
    tables = make_tables(group)
    ids = matches.reshape(-1)
    sigma = sigma_coef[None, :]
    table = gather_all(noisy, grid)
    coeffs, acc, wsum = phase(False, cube_home, ids, sigma, tables, table, group)
    basic = settle(acc, wsum, noisy, grid)
    guide = gather_all(basic, grid)
    acc2, wsum2 = phase(True, cube_home, ids, sigma, tables, guide, group, coeffs)
    return basic, settle(acc2, wsum2, noisy, grid)


def solution(mesh):
    in_specs = (P(("groups", "space"), None), P(("groups", "space"), None), P("groups"), P())
    out_specs = (P(("groups", "space"), None), P(("groups", "space"), None))
    grid = 2 if mesh.shape["groups"] == 2 else 1
    return jax.shard_map(
        functools.partial(body, grid),
        mesh=mesh,
        in_specs=in_specs,
        out_specs=out_specs,
        check_vma=False,
    )
```

```python
import functools

import jax
import jax.numpy as jnp
import numpy as np
from jax import lax
from jax.experimental import pallas as pl
from jax.experimental.pallas import tpu as pltpu
from jax.sharding import PartitionSpec as P

shrink_level = 2.7
prior_weight = 0.5
LANES = 128
CHUNK = 512
ROWS = 384
TOGETHER = 2


def dct_matrix(length):
    index = np.arange(length, dtype=np.float64)
    table = np.cos(np.pi * (2.0 * index[None, :] + 1.0) * index[:, None] / (2.0 * length))
    table = table * np.sqrt(2.0 / length)
    table[0] /= np.sqrt(2.0)
    return table


def split(value):
    high = value.astype(jnp.bfloat16)
    return high, (value - high.astype(jnp.float32)).astype(jnp.bfloat16)


def make_tables(group):
    small = dct_matrix(8)
    cube = np.kron(np.kron(small, small), small).astype(np.float32)
    mix = np.kron(np.eye(LANES // group), dct_matrix(group)).astype(np.float32)
    mixes = [
        np.concatenate([np.asarray(half, np.float32) for half in split(each)], axis=1)
        for each in (mix, mix.T)
    ]
    return (cube.astype(jnp.bfloat16), cube.T.astype(jnp.bfloat16)) + tuple(
        each.astype(jnp.bfloat16) for each in mixes
    )


def mix_rows(table, value):
    both, high = table, table[:, :LANES]
    pieces = []
    for i in range(0, value.shape[0], LANES):
        top, low = split(value[i : i + LANES])
        pieces.append(
            jnp.dot(both, jnp.concatenate([top, top], axis=0), preferred_element_type=jnp.float32)
            + jnp.dot(high, low, preferred_element_type=jnp.float32)
        )
    return jnp.concatenate(pieces, axis=0)


def kernel(second, group, *refs):
    if second:
        (rows_in, sigma, cube, cube_t, mix, mix_t, coeffs, table, acc_out, wsum) = refs[:10]
    else:
        (home, ids, sigma, cube, cube_t, mix, mix_t, table, coeffs, rows_in, acc_out, wsum) = refs[:12]
    big, members, stage, sem = refs[-4:]
    cubes, width = table.shape
    full = big.shape[1]
    groups = members.shape[0]
    entries = groups * group
    chunks = cubes // CHUNK
    steps = entries // ROWS

    def fetch(i, slot):
        rows = pl.ds(pl.multiple_of(i * CHUNK, CHUNK), CHUNK)
        return pltpu.make_async_copy(table.at[rows, :], stage.at[slot], sem.at[slot])

    fetch(0, 0).start()

    def load_step(i, carry):
        slot = lax.rem(i, 2)

        @pl.when(i + 1 < chunks)
        def _():
            fetch(i + 1, 1 - slot).start()

        fetch(i, slot).wait()
        rows = pl.ds(pl.multiple_of(i * CHUNK, CHUNK), CHUNK)
        big[rows, :width] = stage[slot].astype(jnp.float32)
        return carry

    lax.fori_loop(0, chunks, load_step, 0)

    def gather_step(r, carry):
        base = r * group
        places = [rows_in[base + m] if second else home[ids[base + m]] for m in range(group)]
        if not second:
            for m in range(group):
                rows_in[base + m] = places[m]
        picked = [big[pl.ds(places[m], 1), :] for m in range(group)]
        for m in range(group):
            members[r, m : m + 1, :] = picked[m]
        return carry

    lax.fori_loop(0, groups, gather_step, 0)

    noise = sigma[...] * sigma[...]
    level = (shrink_level * sigma[...]) * (shrink_level * sigma[...])

    def compute_step(b, carry):
        rows = pl.ds(pl.multiple_of(b * ROWS, ROWS), ROWS)
        refs_here = ROWS // group
        some = pl.ds(b * refs_here, refs_here)
        taken = members[some, :, :width].reshape(ROWS, width).astype(jnp.bfloat16)
        cleared = cubes // steps
        big[pl.ds(pl.multiple_of(b * cleared, cleared), cleared), :] = jnp.zeros(
            (cleared, full), jnp.float32
        )
        spec = jnp.dot(taken, cube_t[...], preferred_element_type=jnp.float32)
        own = mix_rows(mix[...], spec)
        square = own * own
        if second:
            gain = square / (square + noise)
            energy = gain * gain * noise
            shrunk = gain * coeffs[rows, :]
        else:
            coeffs[rows, :] = own
            gain = square / (square + level)
            energy = gain * gain
            shrunk = gain * own
        total = jnp.sum(jnp.sum(energy, axis=1, keepdims=True).reshape(refs_here, group, 1), axis=1)
        weight = 1.0 / (0.25 + total / (group * width))
        back = mix_rows(mix_t[...], shrunk).astype(jnp.bfloat16)
        out = jnp.dot(back, cube[...], preferred_element_type=jnp.float32)
        each = jnp.broadcast_to(weight[:, None, :], (refs_here, group, 1)).reshape(ROWS, 1)
        part = (each * out).astype(jnp.bfloat16).astype(jnp.float32)
        members[some, :, :width] = part.reshape(refs_here, group, width)
        members[some, :, width:] = jnp.broadcast_to(
            weight[:, None, :].astype(jnp.bfloat16).astype(jnp.float32), (refs_here, group, LANES)
        )
        return carry

    lax.fori_loop(0, steps, compute_step, 0)

    def scatter_step(r, carry):
        base = r * group
        for first in range(0, group, TOGETHER):
            places = [rows_in[base + first + m] for m in range(TOGETHER)]
            added = [members[r, first + m : first + m + 1, :] for m in range(TOGETHER)]
            before = [big[pl.ds(place, 1), :] for place in places]
            for m in range(TOGETHER):
                total = before[m] + added[m]
                for k in range(m):
                    total = total + jnp.where(places[k] == places[m], added[k], 0.0)
                before[m] = total
            for m in range(TOGETHER):
                big[pl.ds(places[m], 1), :] = before[m]
        return carry

    lax.fori_loop(0, groups, scatter_step, 0)

    def put(i, slot):
        rows = pl.ds(pl.multiple_of(i * CHUNK, CHUNK), CHUNK)
        return pltpu.make_async_copy(stage.at[slot], acc_out.at[rows, :], sem.at[slot])

    def store_step(i, carry):
        slot = lax.rem(i, 2)

        @pl.when(i >= 2)
        def _():
            put(i - 2, slot).wait()

        rows = pl.ds(pl.multiple_of(i * CHUNK, CHUNK), CHUNK)
        stage[slot] = big[rows, :width].astype(jnp.bfloat16)
        put(i, slot).start()
        return carry

    lax.fori_loop(0, chunks, store_step, 0)

    lane = lax.broadcasted_iota(jnp.int32, (LANES, LANES), 1)
    sub = lax.broadcasted_iota(jnp.int32, (LANES, LANES), 0)

    def weight_step(i, carry):
        rows = pl.ds(pl.multiple_of(i * LANES, LANES), LANES)
        wsum[pl.ds(i, 1), :] = jnp.sum(
            jnp.where(lane == sub, big[rows, width:], 0.0), axis=0, keepdims=True
        )
        return carry

    lax.fori_loop(0, cubes // LANES, weight_step, 0)
    for i in (chunks - 2, chunks - 1):
        put(i, i % 2).wait()


def phase(second, places, sigma, tables, table, group, coeffs=None):
    cubes, width = table.shape
    entries = places[-1].shape[0]
    vmem = pl.BlockSpec(memory_space=pltpu.VMEM)
    smem = pl.BlockSpec(memory_space=pltpu.SMEM)
    anywhere = pl.BlockSpec(memory_space=pltpu.HBM)
    held = jax.ShapeDtypeStruct((entries, width), jnp.float32)
    outs = [
        jax.ShapeDtypeStruct((cubes, width), jnp.bfloat16),
        jax.ShapeDtypeStruct((cubes // LANES, LANES), jnp.float32),
    ]
    out_specs = [anywhere, vmem]
    in_specs = [smem] * len(places) + [vmem] * 5
    args = [*places, sigma, *tables]
    if second:
        in_specs = in_specs + [vmem, anywhere]
        args = args + [coeffs, table]
    else:
        in_specs = in_specs + [anywhere]
        args = args + [table]
        outs = [held, jax.ShapeDtypeStruct((entries,), jnp.int32)] + outs
        out_specs = [vmem, smem] + out_specs
    return pl.pallas_call(
        functools.partial(kernel, second, group),
        out_shape=outs,
        in_specs=in_specs,
        out_specs=out_specs,
        scratch_shapes=[
            pltpu.VMEM((cubes, width + LANES), jnp.float32),
            pltpu.VMEM((entries // group, group, width + LANES), jnp.float32),
            pltpu.VMEM((2, CHUNK, width), jnp.bfloat16),
            pltpu.SemaphoreType.DMA((2,)),
        ],
        compiler_params=pltpu.CompilerParams(vmem_limit_bytes=60 * 1024 * 1024),
        name="wiener" if second else "shrink",
    )(*args)


MESH = pl.DeviceIdType.MESH


class Ring:
    def __init__(self, grid, count):
        self.grid, self.chips = grid, count // 2
        self.me = lax.axis_index("space")
        self.core = lax.rem(self.me, 2)
        self.spot = self.spot_of(self.me // 2)
        self.partner = {"space": self.me + 1 - 2 * self.core}
        self.sides = tuple({"space": self.device(sign, self.core)} for sign in (1, -1))

    def spot_of(self, chip):
        if self.grid == 1:
            return chip
        side, along = lax.rem(chip, 2), chip // 2
        return along + side * (self.chips - 1 - 2 * along)

    def chip(self, offset):
        spot = lax.rem(self.spot + offset + self.chips, self.chips)
        if self.grid == 1:
            return spot
        side = (2 * spot) // self.chips
        return (spot + side * (self.chips - 1 - 2 * spot)) * 2 + side

    def device(self, offset, core):
        return self.chip(offset) * 2 + core

    def greet(self):
        barrier = pltpu.get_barrier_semaphore()
        for device in (*self.sides, self.partner):
            pl.semaphore_signal(barrier, inc=1, device_id=device, device_id_type=MESH)
        pl.semaphore_wait(barrier, 3)


def hops(chips, pieces):
    far = chips // 2
    orders = []
    for way in range(2):
        halves = range(pieces // 2) if way == 0 else range(pieces // 2, pieces)
        orders.append([(d, j) for d in range(1, far) for j in range(pieces)] + [(far, j) for j in halves])
    return orders


def remote(src, dst, send, recv, device):
    return pltpu.make_async_remote_copy(
        src_ref=src, dst_ref=dst, send_sem=send, recv_sem=recv, device_id=device, device_id_type=MESH
    )


def gather_kernel(grid, x, out, send, recv, give, take, own):
    count, held = out.shape[:2]
    pieces = held // LANES
    ring = Ring(grid, count)
    orders = hops(ring.chips, pieces)
    where = [{key: t for t, key in enumerate(order)} for order in orders]
    last = len(orders[0])
    ring.greet()

    def part(block, j):
        return out.at[block, pl.ds(j * LANES, LANES), :]

    started = []

    def start(copy):
        copy.start()
        started.append(copy)

    for j in range(pieces):
        for way in range(2):
            if (1, j) in where[way]:
                t = where[way][(1, j)]
                start(
                    remote(
                        x.at[pl.ds(j * LANES, LANES), :],
                        part(ring.me, j),
                        send.at[way, t],
                        recv.at[way, t],
                        ring.sides[way],
                    )
                )
    keep = pltpu.make_async_copy(x, out.at[ring.me], own.at[0])
    keep.start()
    start(remote(x, out.at[ring.me], give.at[0, last], take.at[0, last], ring.partner))
    for t in range(last):
        for way in range(2):
            d, j = orders[way][t]
            block = ring.device(-d if way == 0 else d, ring.core)
            piece = part(block, j)
            remote(piece, piece, send.at[way, t], recv.at[way, t], ring.sides[way]).wait_recv()
            onward = where[way].get((d + 1, j))
            if onward is not None:
                start(
                    remote(
                        piece, piece, send.at[way, onward], recv.at[way, onward], ring.sides[way]
                    )
                )
            start(remote(piece, piece, give.at[way, t], take.at[way, t], ring.partner))
    other = ring.me + 1 - 2 * ring.core
    remote(
        out.at[other], out.at[other], give.at[0, last], take.at[0, last], ring.partner
    ).wait_recv()
    for t in range(last):
        for way in range(2):
            d, j = orders[way][t]
            piece = part(ring.device(-d if way == 0 else d, 1 - ring.core), j)
            remote(piece, piece, give.at[way, t], take.at[way, t], ring.partner).wait_recv()
    for copy in started:
        copy.wait_send()
    keep.wait()


def gather_all(x, grid):
    count = lax.axis_size("space")
    held, width = x.shape
    last = len(hops(count // 2, held // LANES)[0])
    sems = pltpu.SemaphoreType.DMA
    out = pl.pallas_call(
        functools.partial(gather_kernel, grid),
        out_shape=jax.ShapeDtypeStruct((count, held, width), x.dtype),
        in_specs=[pl.BlockSpec(memory_space=pltpu.VMEM)],
        out_specs=pl.BlockSpec(memory_space=pltpu.HBM),
        scratch_shapes=[
            sems((2, last)),
            sems((2, last)),
            sems((2, last + 1)),
            sems((2, last + 1)),
            sems((1,)),
        ],
        compiler_params=pltpu.CompilerParams(collective_id=0, has_side_effects=True),
        name="spread",
    )(x)
    return out.reshape(count * held, width)


def reduce_kernel(grid, acc, wsum, noisy, out, own, other, got, sent, wother, wgot, wsent, *sems):
    own_sem, give, take, send, recv, wgive, wtake, wsend, wrecv = sems
    chips = acc.shape[0]
    pieces = acc.shape[2] // LANES
    ring = Ring(grid, 2 * chips)
    far = chips // 2
    orders = [
        sorted(order, key=lambda key: (-key[0], key[1])) for order in hops(chips, pieces)
    ]
    where = [{key: t for t, key in enumerate(order)} for order in orders]
    last = len(orders[0])
    offsets = [far] + [s * d for d in range(far - 1, 0, -1) for s in (1, -1)] + [0]
    slot_of = {off: i for i, off in enumerate(offsets)}
    slot_of[-far] = 0
    started, local, gifts = [], [], []

    for i, off in enumerate(offsets):
        copy = pltpu.make_async_copy(acc.at[ring.chip(off), ring.core], own.at[i], own_sem.at[i])
        copy.start()
        local.append(copy)
    ring.greet()
    for i, off in enumerate(offsets):
        copy = remote(
            acc.at[ring.chip(off), 1 - ring.core], other.at[i], give.at[i], take.at[i], ring.partner
        )
        copy.start()
        gifts.append(copy)
        if i == 0:
            wgift = remote(wsum, wother, wgive.at[0], wtake.at[0], ring.partner)
            wgift.start()
    ready = set()

    def settle_slot(i):
        if i not in ready:
            ready.add(i)
            local[i].wait()
            gifts[i].wait_recv()

    def value(off, j, ways, d):
        i = slot_of[off]
        settle_slot(i)
        rows = pl.ds(j * LANES, LANES)
        total = own[i, rows, :].astype(jnp.float32) + other[i, rows, :].astype(jnp.float32)
        for way in ways:
            t = where[way].get((d + 1, j))
            if t is not None:
                piece = got.at[way, t]
                remote(sent.at[way, t], piece, send.at[way, t], recv.at[way, t], ring.sides[way]).wait_recv()
                total = total + piece[...].astype(jnp.float32)
        return total

    def weights(off, ways, d):
        chip = ring.chip(off)
        if "w" not in ready:
            ready.add("w")
            wgift.wait_recv()
        total = wsum[chip, ring.core] + wother[chip, ring.core]
        for way in ways:
            if d + 1 < far or (d + 1 == far and way == 0):
                remote(
                    wsent.at[way, d + 1],
                    wgot.at[way, d + 1],
                    wsend.at[way, d + 1],
                    wrecv.at[way, d + 1],
                    ring.sides[way],
                ).wait_recv()
                total = total + wgot[way, d + 1]
        return total

    for t in range(last):
        for way in range(2):
            d, j = orders[way][t]
            off = d if way == 0 else -d
            sent[way, t] = value(off, j, (way,), d).astype(sent.dtype)
            copy = remote(sent.at[way, t], got.at[way, t], send.at[way, t], recv.at[way, t], ring.sides[way])
            copy.start()
            started.append(copy)
            final_piece = t + 1 == last or orders[way][t + 1][0] != d
            if final_piece and (d < far or way == 0):
                wsent[way, d] = weights(off, (way,), d)
                copy = remote(
                    wsent.at[way, d], wgot.at[way, d], wsend.at[way, d], wrecv.at[way, d], ring.sides[way]
                )
                copy.start()
                started.append(copy)
    lane = lax.broadcasted_iota(jnp.int32, (LANES, LANES), 1)
    sub = lax.broadcasted_iota(jnp.int32, (LANES, LANES), 0)
    denom = weights(0, (0, 1), 0)
    for j in range(pieces):
        rows = pl.ds(j * LANES, LANES)
        numer = value(0, j, (0, 1), 0) + prior_weight * noisy[rows, :].astype(jnp.float32)
        spread = jnp.broadcast_to(denom[j : j + 1, :], (LANES, LANES))
        column = jnp.sum(jnp.where(lane == sub, spread, 0.0), axis=1, keepdims=True)
        out[rows, :] = (numer / (column + prior_weight)).astype(out.dtype)
    for copy in started + gifts + [wgift]:
        copy.wait_send()


def settle(acc, wsum, noisy, grid):
    count = lax.axis_size("space")
    held, width = noisy.shape
    chips, pieces = count // 2, held // LANES
    far = chips // 2
    last = len(hops(chips, pieces)[0])
    sems = pltpu.SemaphoreType.DMA
    vmem = pl.BlockSpec(memory_space=pltpu.VMEM)
    small = (chips, 2, pieces, LANES)
    return pl.pallas_call(
        functools.partial(reduce_kernel, grid),
        out_shape=jax.ShapeDtypeStruct(noisy.shape, noisy.dtype),
        in_specs=[pl.BlockSpec(memory_space=pltpu.HBM), vmem, vmem],
        out_specs=vmem,
        scratch_shapes=[
            pltpu.VMEM((chips, held, width), acc.dtype),
            pltpu.VMEM((chips, held, width), acc.dtype),
            pltpu.VMEM((2, last, LANES, width), acc.dtype),
            pltpu.VMEM((2, last, LANES, width), acc.dtype),
            pltpu.VMEM(small, jnp.float32),
            pltpu.VMEM((2, far + 1, pieces, LANES), jnp.float32),
            pltpu.VMEM((2, far + 1, pieces, LANES), jnp.float32),
            sems((chips,)),
            sems((chips,)),
            sems((chips,)),
            sems((2, last)),
            sems((2, last)),
            sems((1,)),
            sems((1,)),
            sems((2, far + 1)),
            sems((2, far + 1)),
        ],
        compiler_params=pltpu.CompilerParams(
            collective_id=1, has_side_effects=True, vmem_limit_bytes=60 * 1024 * 1024
        ),
        name="settle",
    )(acc.reshape(chips, 2, held, width), wsum.reshape(small), noisy)


def body(grid, noisy, matches, cube_home, sigma_coef):
    group = matches.shape[1]
    tables = make_tables(group)
    ids = matches.reshape(-1)
    sigma = sigma_coef[None, :]
    table = gather_all(noisy, grid)
    coeffs, rows, acc, wsum = phase(False, (cube_home, ids), sigma, tables, table, group)
    basic = settle(acc, wsum, noisy, grid)
    guide = gather_all(basic, grid)
    acc2, wsum2 = phase(True, (rows,), sigma, tables, guide, group, coeffs)
    return basic, settle(acc2, wsum2, noisy, grid)


def solution(mesh):
    in_specs = (P(("groups", "space"), None), P(("groups", "space"), None), P("groups"), P())
    out_specs = (P(("groups", "space"), None), P(("groups", "space"), None))
    grid = 2 if mesh.shape["groups"] == 2 else 1
    return jax.shard_map(
        functools.partial(body, grid),
        mesh=mesh,
        in_specs=in_specs,
        out_specs=out_specs,
        check_vma=False,
    )
```

```python
import functools

import jax
import jax.numpy as jnp
import numpy as np
from jax import lax
from jax.experimental import pallas as pl
from jax.experimental.pallas import tpu as pltpu
from jax.sharding import PartitionSpec as P

shrink_level = 2.7
prior_weight = 0.5
LANES = 128
CHUNK = 512
ROWS = 384
TOGETHER = 2
LAG = 3


def dct_matrix(length):
    index = np.arange(length, dtype=np.float64)
    table = np.cos(np.pi * (2.0 * index[None, :] + 1.0) * index[:, None] / (2.0 * length))
    table = table * np.sqrt(2.0 / length)
    table[0] /= np.sqrt(2.0)
    return table


def split(value):
    high = value.astype(jnp.bfloat16)
    return high, (value - high.astype(jnp.float32)).astype(jnp.bfloat16)


def make_tables(group):
    small = dct_matrix(8)
    cube = np.kron(np.kron(small, small), small).astype(np.float32)
    mix = np.kron(np.eye(LANES // group), dct_matrix(group)).astype(np.float32)
    mixes = [
        np.concatenate([np.asarray(half, np.float32) for half in split(each)], axis=1)
        for each in (mix, mix.T)
    ]
    return (cube.astype(jnp.bfloat16), cube.T.astype(jnp.bfloat16)) + tuple(
        each.astype(jnp.bfloat16) for each in mixes
    )


def mix_rows(table, value):
    both, high = table, table[:, :LANES]
    pieces = []
    for i in range(0, value.shape[0], LANES):
        top, low = split(value[i : i + LANES])
        pieces.append(
            jnp.dot(both, jnp.concatenate([top, top], axis=0), preferred_element_type=jnp.float32)
            + jnp.dot(high, low, preferred_element_type=jnp.float32)
        )
    return jnp.concatenate(pieces, axis=0)


def kernel(second, group, *refs):
    rows_in, sigma, cube, cube_t, mix, mix_t, taken_in, coeffs, acc_out, wsum = refs[:10]
    big, members, stage, sem = refs[-4:]
    cubes, width = acc_out.shape
    full = big.shape[1]
    groups = members.shape[0]
    entries = groups * group
    chunks = cubes // CHUNK
    steps = entries // ROWS

    noise = sigma[...] * sigma[...]
    level = (shrink_level * sigma[...]) * (shrink_level * sigma[...])

    def compute_step(b, carry):
        rows = pl.ds(pl.multiple_of(b * ROWS, ROWS), ROWS)
        refs_here = ROWS // group
        some = pl.ds(b * refs_here, refs_here)
        cleared = cubes // steps
        big[pl.ds(pl.multiple_of(b * cleared, cleared), cleared), :] = jnp.zeros(
            (cleared, full), jnp.float32
        )
        spec = jnp.dot(taken_in[rows, :], cube_t[...], preferred_element_type=jnp.float32)
        own = mix_rows(mix[...], spec)
        square = own * own
        if second:
            gain = square / (square + noise)
            energy = gain * gain * noise
            shrunk = gain * coeffs[rows, :]
        else:
            coeffs[rows, :] = own
            gain = square / (square + level)
            energy = gain * gain
            shrunk = gain * own
        total = jnp.sum(jnp.sum(energy, axis=1, keepdims=True).reshape(refs_here, group, 1), axis=1)
        weight = 1.0 / (0.25 + total / (group * width))
        back = mix_rows(mix_t[...], shrunk).astype(jnp.bfloat16)
        out = jnp.dot(back, cube[...], preferred_element_type=jnp.float32)
        each = jnp.broadcast_to(weight[:, None, :], (refs_here, group, 1)).reshape(ROWS, 1)
        part = (each * out).astype(jnp.bfloat16).astype(jnp.float32)
        members[some, :, :width] = part.reshape(refs_here, group, width)
        members[some, :, width:] = jnp.broadcast_to(
            weight[:, None, :].astype(jnp.bfloat16).astype(jnp.float32), (refs_here, group, LANES)
        )
        return carry

    lax.fori_loop(0, steps, compute_step, 0)

    def scatter_step(r, carry):
        base = r * group
        for first in range(0, group, TOGETHER):
            places = [rows_in[base + first + m] for m in range(TOGETHER)]
            added = [members[r, first + m : first + m + 1, :] for m in range(TOGETHER)]
            before = [big[pl.ds(place, 1), :] for place in places]
            for m in range(TOGETHER):
                total = before[m] + added[m]
                for k in range(m):
                    total = total + jnp.where(places[k] == places[m], added[k], 0.0)
                before[m] = total
            for m in range(TOGETHER):
                big[pl.ds(places[m], 1), :] = before[m]
        return carry

    lax.fori_loop(0, groups, scatter_step, 0)

    def put(i, slot):
        rows = pl.ds(pl.multiple_of(i * CHUNK, CHUNK), CHUNK)
        return pltpu.make_async_copy(stage.at[slot], acc_out.at[rows, :], sem.at[slot])

    def store_step(i, carry):
        slot = lax.rem(i, 2)

        @pl.when(i >= 2)
        def _():
            put(i - 2, slot).wait()

        rows = pl.ds(pl.multiple_of(i * CHUNK, CHUNK), CHUNK)
        stage[slot] = big[rows, :width].astype(jnp.bfloat16)
        put(i, slot).start()
        return carry

    lax.fori_loop(0, chunks, store_step, 0)

    lane = lax.broadcasted_iota(jnp.int32, (LANES, LANES), 1)
    sub = lax.broadcasted_iota(jnp.int32, (LANES, LANES), 0)

    def weight_step(i, carry):
        rows = pl.ds(pl.multiple_of(i * LANES, LANES), LANES)
        wsum[pl.ds(i, 1), :] = jnp.sum(
            jnp.where(lane == sub, big[rows, width:], 0.0), axis=0, keepdims=True
        )
        return carry

    lax.fori_loop(0, cubes // LANES, weight_step, 0)
    for i in (chunks - 2, chunks - 1):
        put(i, i % 2).wait()


def phase(second, places, sigma, tables, taken, cubes, group, coeffs=None):
    entries, width = taken.shape
    vmem = pl.BlockSpec(memory_space=pltpu.VMEM)
    smem = pl.BlockSpec(memory_space=pltpu.SMEM)
    held = jax.ShapeDtypeStruct((entries, width), jnp.float32)
    outs = [
        jax.ShapeDtypeStruct((cubes, width), jnp.bfloat16),
        jax.ShapeDtypeStruct((cubes // LANES, LANES), jnp.float32),
    ]
    out_specs = [pl.BlockSpec(memory_space=pltpu.HBM), vmem]
    in_specs = [smem] + [vmem] * 6
    args = [places, sigma, *tables, taken]
    if second:
        in_specs = in_specs + [vmem]
        args = args + [coeffs]
    else:
        outs = [held] + outs
        out_specs = [vmem] + out_specs
    return pl.pallas_call(
        functools.partial(kernel, second, group),
        out_shape=outs,
        in_specs=in_specs,
        out_specs=out_specs,
        scratch_shapes=[
            pltpu.VMEM((cubes, width + LANES), jnp.float32),
            pltpu.VMEM((entries // group, group, width + LANES), jnp.float32),
            pltpu.VMEM((2, CHUNK, width), jnp.bfloat16),
            pltpu.SemaphoreType.DMA((2,)),
        ],
        compiler_params=pltpu.CompilerParams(vmem_limit_bytes=60 * 1024 * 1024),
        name="wiener" if second else "shrink",
    )(*args)


MESH = pl.DeviceIdType.MESH


class Ring:
    def __init__(self, grid, count):
        self.grid, self.chips = grid, count // 2
        self.me = lax.axis_index("space")
        self.core = lax.rem(self.me, 2)
        self.spot = self.spot_of(self.me // 2)
        self.partner = {"space": self.me + 1 - 2 * self.core}
        self.sides = tuple({"space": self.device(sign, self.core)} for sign in (1, -1))

    def spot_of(self, chip):
        if self.grid == 1:
            return chip
        side, along = lax.rem(chip, 2), chip // 2
        return along + side * (self.chips - 1 - 2 * along)

    def chip(self, offset):
        spot = lax.rem(self.spot + offset + self.chips, self.chips)
        if self.grid == 1:
            return spot
        side = (2 * spot) // self.chips
        return (spot + side * (self.chips - 1 - 2 * spot)) * 2 + side

    def device(self, offset, core):
        return self.chip(offset) * 2 + core

    def greet(self):
        barrier = pltpu.get_barrier_semaphore()
        for device in (*self.sides, self.partner):
            pl.semaphore_signal(barrier, inc=1, device_id=device, device_id_type=MESH)
        pl.semaphore_wait(barrier, 3)


def hops(chips, pieces):
    far = chips // 2
    orders = []
    for way in range(2):
        halves = range(pieces // 2) if way == 0 else range(pieces // 2, pieces)
        orders.append([(d, j) for d in range(1, far) for j in range(pieces)] + [(far, j) for j in halves])
    return orders


def remote(src, dst, send, recv, device):
    return pltpu.make_async_remote_copy(
        src_ref=src, dst_ref=dst, send_sem=send, recv_sem=recv, device_id=device, device_id_type=MESH
    )


def gather_kernel(grid, second, *refs):
    if second:
        x, places, taken = refs[:3]
    else:
        x, home, ids, taken, places = refs[:5]
    held_in, big, members, send, recv, give, take = refs[-7:]
    count, held = held_in.shape[:2]
    groups, group = members.shape[:2]
    width = x.shape[1]
    pieces = held // LANES
    ring = Ring(grid, count)
    orders = hops(ring.chips, pieces)
    where = [{key: t for t, key in enumerate(order)} for order in orders]
    last = len(orders[0])
    ring.greet()

    def part(block, j):
        return held_in.at[block, pl.ds(j * LANES, LANES), :]

    def widen(block, j, source):
        rows = pl.ds(pl.multiple_of(block * held + j * LANES, LANES), LANES)
        big[rows, :] = source[...].astype(jnp.float32)

    started = []

    def start(copy):
        copy.start()
        started.append(copy)

    for j in range(pieces):
        for way in range(2):
            if (1, j) in where[way]:
                t = where[way][(1, j)]
                start(
                    remote(
                        x.at[pl.ds(j * LANES, LANES), :],
                        part(ring.me, j),
                        send.at[way, t],
                        recv.at[way, t],
                        ring.sides[way],
                    )
                )
    start(remote(x, held_in.at[ring.me], give.at[0, last], take.at[0, last], ring.partner))
    for j in range(pieces):
        widen(ring.me, j, x.at[pl.ds(j * LANES, LANES), :])
    other = ring.me + 1 - 2 * ring.core

    def accept(t):
        for way in range(2):
            d, j = orders[way][t]
            block = ring.device(-d if way == 0 else d, 1 - ring.core)
            piece = part(block, j)
            remote(piece, piece, give.at[way, t], take.at[way, t], ring.partner).wait_recv()
            widen(block, j, piece)

    for t in range(last):
        for way in range(2):
            d, j = orders[way][t]
            block = ring.device(-d if way == 0 else d, ring.core)
            piece = part(block, j)
            remote(piece, piece, send.at[way, t], recv.at[way, t], ring.sides[way]).wait_recv()
            onward = where[way].get((d + 1, j))
            if onward is not None:
                start(
                    remote(
                        piece, piece, send.at[way, onward], recv.at[way, onward], ring.sides[way]
                    )
                )
            start(remote(piece, piece, give.at[way, t], take.at[way, t], ring.partner))
            widen(block, j, piece)
        if t == 2:
            remote(
                held_in.at[other], held_in.at[other], give.at[0, last], take.at[0, last], ring.partner
            ).wait_recv()
            for j in range(pieces):
                widen(other, j, part(other, j))
        if t >= LAG:
            accept(t - LAG)
    for t in range(last - LAG, last):
        accept(t)

    def gather_step(r, carry):
        base = r * group
        spots = [places[base + m] if second else home[ids[base + m]] for m in range(group)]
        if not second:
            for m in range(group):
                places[base + m] = spots[m]
        picked = [big[pl.ds(spots[m], 1), :] for m in range(group)]
        for m in range(group):
            members[r, m : m + 1, :] = picked[m]
        return carry

    lax.fori_loop(0, groups, gather_step, 0)

    def narrow_step(b, carry):
        some = LANES // group
        rows = pl.ds(pl.multiple_of(b * LANES, LANES), LANES)
        taken[rows, :] = members[pl.ds(b * some, some)].reshape(LANES, width).astype(taken.dtype)
        return carry

    lax.fori_loop(0, groups * group // LANES, narrow_step, 0)
    for copy in started:
        copy.wait_send()


def gather_rows(x, lists, grid, groups, group):
    count = lax.axis_size("space")
    held, width = x.shape
    entries = groups * group
    last = len(hops(count // 2, held // LANES)[0])
    sems = pltpu.SemaphoreType.DMA
    second = len(lists) == 1
    vmem = pl.BlockSpec(memory_space=pltpu.VMEM)
    smem = pl.BlockSpec(memory_space=pltpu.SMEM)
    outs = [jax.ShapeDtypeStruct((entries, width), x.dtype)]
    out_specs = [vmem]
    if not second:
        outs.append(jax.ShapeDtypeStruct((entries,), jnp.int32))
        out_specs.append(smem)
    return pl.pallas_call(
        functools.partial(gather_kernel, grid, second),
        out_shape=outs,
        in_specs=[vmem] + [smem] * len(lists),
        out_specs=out_specs,
        scratch_shapes=[
            pltpu.VMEM((count, held, width), x.dtype),
            pltpu.VMEM((count * held, width), jnp.float32),
            pltpu.VMEM((groups, group, width), jnp.float32),
            sems((2, last)),
            sems((2, last)),
            sems((2, last + 1)),
            sems((2, last + 1)),
        ],
        compiler_params=pltpu.CompilerParams(
            collective_id=2 if second else 0,
            has_side_effects=True,
            vmem_limit_bytes=60 * 1024 * 1024,
        ),
        name="spread",
    )(x, *lists)


def reduce_kernel(grid, acc, wsum, noisy, out, own, other, got, sent, wother, wgot, wsent, *sems):
    own_sem, give, take, send, recv, wgive, wtake, wsend, wrecv = sems
    chips = acc.shape[0]
    pieces = acc.shape[2] // LANES
    ring = Ring(grid, 2 * chips)
    far = chips // 2
    orders = [
        sorted(order, key=lambda key: (-key[0], key[1])) for order in hops(chips, pieces)
    ]
    where = [{key: t for t, key in enumerate(order)} for order in orders]
    last = len(orders[0])
    offsets = [far] + [s * d for d in range(far - 1, 0, -1) for s in (1, -1)] + [0]
    slot_of = {off: i for i, off in enumerate(offsets)}
    slot_of[-far] = 0
    started, local, gifts = [], [], []

    for i, off in enumerate(offsets):
        copy = pltpu.make_async_copy(acc.at[ring.chip(off), ring.core], own.at[i], own_sem.at[i])
        copy.start()
        local.append(copy)
    ring.greet()
    for i, off in enumerate(offsets):
        copy = remote(
            acc.at[ring.chip(off), 1 - ring.core], other.at[i], give.at[i], take.at[i], ring.partner
        )
        copy.start()
        gifts.append(copy)
        if i == 0:
            wgift = remote(wsum, wother, wgive.at[0], wtake.at[0], ring.partner)
            wgift.start()
    ready = set()

    def settle_slot(i):
        if i not in ready:
            ready.add(i)
            local[i].wait()
            gifts[i].wait_recv()

    def value(off, j, ways, d):
        i = slot_of[off]
        settle_slot(i)
        rows = pl.ds(j * LANES, LANES)
        total = own[i, rows, :].astype(jnp.float32) + other[i, rows, :].astype(jnp.float32)
        for way in ways:
            t = where[way].get((d + 1, j))
            if t is not None:
                piece = got.at[way, t]
                remote(sent.at[way, t], piece, send.at[way, t], recv.at[way, t], ring.sides[way]).wait_recv()
                total = total + piece[...].astype(jnp.float32)
        return total

    def weights(off, ways, d):
        chip = ring.chip(off)
        if "w" not in ready:
            ready.add("w")
            wgift.wait_recv()
        total = wsum[chip, ring.core] + wother[chip, ring.core]
        for way in ways:
            if d + 1 < far or (d + 1 == far and way == 0):
                remote(
                    wsent.at[way, d + 1],
                    wgot.at[way, d + 1],
                    wsend.at[way, d + 1],
                    wrecv.at[way, d + 1],
                    ring.sides[way],
                ).wait_recv()
                total = total + wgot[way, d + 1]
        return total

    for t in range(last):
        for way in range(2):
            d, j = orders[way][t]
            off = d if way == 0 else -d
            sent[way, t] = value(off, j, (way,), d).astype(sent.dtype)
            copy = remote(sent.at[way, t], got.at[way, t], send.at[way, t], recv.at[way, t], ring.sides[way])
            copy.start()
            started.append(copy)
            final_piece = t + 1 == last or orders[way][t + 1][0] != d
            if final_piece and (d < far or way == 0):
                wsent[way, d] = weights(off, (way,), d)
                copy = remote(
                    wsent.at[way, d], wgot.at[way, d], wsend.at[way, d], wrecv.at[way, d], ring.sides[way]
                )
                copy.start()
                started.append(copy)
    lane = lax.broadcasted_iota(jnp.int32, (LANES, LANES), 1)
    sub = lax.broadcasted_iota(jnp.int32, (LANES, LANES), 0)
    denom = weights(0, (0, 1), 0)
    for j in range(pieces):
        rows = pl.ds(j * LANES, LANES)
        numer = value(0, j, (0, 1), 0) + prior_weight * noisy[rows, :].astype(jnp.float32)
        spread = jnp.broadcast_to(denom[j : j + 1, :], (LANES, LANES))
        column = jnp.sum(jnp.where(lane == sub, spread, 0.0), axis=1, keepdims=True)
        out[rows, :] = (numer / (column + prior_weight)).astype(out.dtype)
    for copy in started + gifts + [wgift]:
        copy.wait_send()


def settle(acc, wsum, noisy, grid):
    count = lax.axis_size("space")
    held, width = noisy.shape
    chips, pieces = count // 2, held // LANES
    far = chips // 2
    last = len(hops(chips, pieces)[0])
    sems = pltpu.SemaphoreType.DMA
    vmem = pl.BlockSpec(memory_space=pltpu.VMEM)
    small = (chips, 2, pieces, LANES)
    return pl.pallas_call(
        functools.partial(reduce_kernel, grid),
        out_shape=jax.ShapeDtypeStruct(noisy.shape, noisy.dtype),
        in_specs=[pl.BlockSpec(memory_space=pltpu.HBM), vmem, vmem],
        out_specs=vmem,
        scratch_shapes=[
            pltpu.VMEM((chips, held, width), acc.dtype),
            pltpu.VMEM((chips, held, width), acc.dtype),
            pltpu.VMEM((2, last, LANES, width), acc.dtype),
            pltpu.VMEM((2, last, LANES, width), acc.dtype),
            pltpu.VMEM(small, jnp.float32),
            pltpu.VMEM((2, far + 1, pieces, LANES), jnp.float32),
            pltpu.VMEM((2, far + 1, pieces, LANES), jnp.float32),
            sems((chips,)),
            sems((chips,)),
            sems((chips,)),
            sems((2, last)),
            sems((2, last)),
            sems((1,)),
            sems((1,)),
            sems((2, far + 1)),
            sems((2, far + 1)),
        ],
        compiler_params=pltpu.CompilerParams(
            collective_id=1, has_side_effects=True, vmem_limit_bytes=60 * 1024 * 1024
        ),
        name="settle",
    )(acc.reshape(chips, 2, held, width), wsum.reshape(small), noisy)


def body(grid, noisy, matches, cube_home, sigma_coef):
    groups, group = matches.shape
    cubes = cube_home.shape[0]
    tables = make_tables(group)
    sigma = sigma_coef[None, :]
    members, rows = gather_rows(noisy, (cube_home, matches.reshape(-1)), grid, groups, group)
    coeffs, acc, wsum = phase(False, rows, sigma, tables, members, cubes, group)
    basic = settle(acc, wsum, noisy, grid)
    (guide,) = gather_rows(basic, (rows,), grid, groups, group)
    acc2, wsum2 = phase(True, rows, sigma, tables, guide, cubes, group, coeffs)
    return basic, settle(acc2, wsum2, noisy, grid)


def solution(mesh):
    in_specs = (P(("groups", "space"), None), P(("groups", "space"), None), P("groups"), P())
    out_specs = (P(("groups", "space"), None), P(("groups", "space"), None))
    grid = 2 if mesh.shape["groups"] == 2 else 1
    return jax.shard_map(
        functools.partial(body, grid),
        mesh=mesh,
        in_specs=in_specs,
        out_specs=out_specs,
        check_vma=False,
    )
```

```python
import functools

import jax
import jax.numpy as jnp
import numpy as np
from jax import lax
from jax.experimental import pallas as pl
from jax.experimental.pallas import tpu as pltpu
from jax.sharding import PartitionSpec as P

shrink_level = 2.7
prior_weight = 0.5
LANES = 128
CHUNK = 512
ROWS = 384
TOGETHER = 2
LAG = 3


def dct_matrix(length):
    index = np.arange(length, dtype=np.float64)
    table = np.cos(np.pi * (2.0 * index[None, :] + 1.0) * index[:, None] / (2.0 * length))
    table = table * np.sqrt(2.0 / length)
    table[0] /= np.sqrt(2.0)
    return table


def split(value):
    high = value.astype(jnp.bfloat16)
    return high, (value - high.astype(jnp.float32)).astype(jnp.bfloat16)


def make_tables(group):
    small = dct_matrix(8)
    cube = np.kron(np.kron(small, small), small).astype(np.float32)
    mix = np.kron(np.eye(LANES // group), dct_matrix(group)).astype(np.float32)
    mixes = [
        np.concatenate([np.asarray(half, np.float32) for half in split(each)], axis=1)
        for each in (mix, mix.T)
    ]
    return (cube.astype(jnp.bfloat16), cube.T.astype(jnp.bfloat16)) + tuple(
        each.astype(jnp.bfloat16) for each in mixes
    )


def mix_rows(table, value):
    both, high = table, table[:, :LANES]
    pieces = []
    for i in range(0, value.shape[0], LANES):
        top, low = split(value[i : i + LANES])
        pieces.append(
            jnp.dot(both, jnp.concatenate([top, top], axis=0), preferred_element_type=jnp.float32)
            + jnp.dot(high, low, preferred_element_type=jnp.float32)
        )
    return jnp.concatenate(pieces, axis=0)


def kernel(second, group, *refs):
    rows_in, sigma, cube, cube_t, mix, mix_t, taken_in, coeffs, acc_out, wsum = refs[:10]
    big, members, stage, sem = refs[-4:]
    cubes, width = acc_out.shape
    full = big.shape[1]
    groups = members.shape[0]
    entries = groups * group
    chunks = cubes // CHUNK
    steps = entries // ROWS

    noise = sigma[...] * sigma[...]
    level = (shrink_level * sigma[...]) * (shrink_level * sigma[...])

    def compute_step(b, carry):
        rows = pl.ds(pl.multiple_of(b * ROWS, ROWS), ROWS)
        refs_here = ROWS // group
        some = pl.ds(b * refs_here, refs_here)
        cleared = cubes // steps
        big[pl.ds(pl.multiple_of(b * cleared, cleared), cleared), :] = jnp.zeros(
            (cleared, full), jnp.float32
        )
        spec = jnp.dot(taken_in[rows, :], cube_t[...], preferred_element_type=jnp.float32)
        own = mix_rows(mix[...], spec)
        square = own * own
        if second:
            gain = square / (square + noise)
            energy = gain * gain * noise
            shrunk = gain * coeffs[rows, :]
        else:
            coeffs[rows, :] = own
            gain = square / (square + level)
            energy = gain * gain
            shrunk = gain * own
        total = jnp.sum(jnp.sum(energy, axis=1, keepdims=True).reshape(refs_here, group, 1), axis=1)
        weight = 1.0 / (0.25 + total / (group * width))
        back = mix_rows(mix_t[...], shrunk).astype(jnp.bfloat16)
        out = jnp.dot(back, cube[...], preferred_element_type=jnp.float32)
        each = jnp.broadcast_to(weight[:, None, :], (refs_here, group, 1)).reshape(ROWS, 1)
        part = (each * out).astype(jnp.bfloat16).astype(jnp.float32)
        members[some, :, :width] = part.reshape(refs_here, group, width)
        members[some, :, width:] = jnp.broadcast_to(
            weight[:, None, :].astype(jnp.bfloat16).astype(jnp.float32), (refs_here, group, LANES)
        )
        return carry

    lax.fori_loop(0, steps, compute_step, 0)

    def scatter_step(r, carry):
        base = r * group
        for first in range(0, group, TOGETHER):
            places = [rows_in[base + first + m] for m in range(TOGETHER)]
            added = [members[r, first + m : first + m + 1, :] for m in range(TOGETHER)]
            before = [big[pl.ds(place, 1), :] for place in places]
            for m in range(TOGETHER):
                total = before[m] + added[m]
                for k in range(m):
                    total = total + jnp.where(places[k] == places[m], added[k], 0.0)
                before[m] = total
            for m in range(TOGETHER):
                big[pl.ds(places[m], 1), :] = before[m]
        return carry

    lax.fori_loop(0, groups, scatter_step, 0, unroll=2)

    def put(i, slot):
        rows = pl.ds(pl.multiple_of(i * CHUNK, CHUNK), CHUNK)
        return pltpu.make_async_copy(stage.at[slot], acc_out.at[rows, :], sem.at[slot])

    def store_step(i, carry):
        slot = lax.rem(i, 2)

        @pl.when(i >= 2)
        def _():
            put(i - 2, slot).wait()

        rows = pl.ds(pl.multiple_of(i * CHUNK, CHUNK), CHUNK)
        stage[slot] = big[rows, :width].astype(jnp.bfloat16)
        put(i, slot).start()
        return carry

    lax.fori_loop(0, chunks, store_step, 0)

    lane = lax.broadcasted_iota(jnp.int32, (LANES, LANES), 1)
    sub = lax.broadcasted_iota(jnp.int32, (LANES, LANES), 0)

    def weight_step(i, carry):
        rows = pl.ds(pl.multiple_of(i * LANES, LANES), LANES)
        wsum[pl.ds(i, 1), :] = jnp.sum(
            jnp.where(lane == sub, big[rows, width:], 0.0), axis=0, keepdims=True
        )
        return carry

    lax.fori_loop(0, cubes // LANES, weight_step, 0, unroll=4)
    for i in (chunks - 2, chunks - 1):
        put(i, i % 2).wait()


def phase(second, places, sigma, tables, taken, cubes, group, coeffs=None):
    entries, width = taken.shape
    vmem = pl.BlockSpec(memory_space=pltpu.VMEM)
    smem = pl.BlockSpec(memory_space=pltpu.SMEM)
    held = jax.ShapeDtypeStruct((entries, width), jnp.float32)
    outs = [
        jax.ShapeDtypeStruct((cubes, width), jnp.bfloat16),
        jax.ShapeDtypeStruct((cubes // LANES, LANES), jnp.float32),
    ]
    out_specs = [pl.BlockSpec(memory_space=pltpu.HBM), vmem]
    in_specs = [smem] + [vmem] * 6
    args = [places, sigma, *tables, taken]
    if second:
        in_specs = in_specs + [vmem]
        args = args + [coeffs]
    else:
        outs = [held] + outs
        out_specs = [vmem] + out_specs
    return pl.pallas_call(
        functools.partial(kernel, second, group),
        out_shape=outs,
        in_specs=in_specs,
        out_specs=out_specs,
        scratch_shapes=[
            pltpu.VMEM((cubes, width + LANES), jnp.float32),
            pltpu.VMEM((entries // group, group, width + LANES), jnp.float32),
            pltpu.VMEM((2, CHUNK, width), jnp.bfloat16),
            pltpu.SemaphoreType.DMA((2,)),
        ],
        compiler_params=pltpu.CompilerParams(vmem_limit_bytes=60 * 1024 * 1024),
        name="wiener" if second else "shrink",
    )(*args)


MESH = pl.DeviceIdType.MESH


class Ring:
    def __init__(self, grid, count):
        self.grid, self.chips = grid, count // 2
        self.me = lax.axis_index("space")
        self.core = lax.rem(self.me, 2)
        self.spot = self.spot_of(self.me // 2)
        self.partner = {"space": self.me + 1 - 2 * self.core}
        self.sides = tuple({"space": self.device(sign, self.core)} for sign in (1, -1))

    def spot_of(self, chip):
        if self.grid == 1:
            return chip
        side, along = lax.rem(chip, 2), chip // 2
        return along + side * (self.chips - 1 - 2 * along)

    def chip(self, offset):
        spot = lax.rem(self.spot + offset + self.chips, self.chips)
        if self.grid == 1:
            return spot
        side = (2 * spot) // self.chips
        return (spot + side * (self.chips - 1 - 2 * spot)) * 2 + side

    def device(self, offset, core):
        return self.chip(offset) * 2 + core

    def greet(self):
        barrier = pltpu.get_barrier_semaphore()
        for device in (*self.sides, self.partner):
            pl.semaphore_signal(barrier, inc=1, device_id=device, device_id_type=MESH)
        pl.semaphore_wait(barrier, 3)


def hops(chips, pieces):
    far = chips // 2
    orders = []
    for way in range(2):
        halves = range(pieces // 2) if way == 0 else range(pieces // 2, pieces)
        orders.append([(d, j) for d in range(1, far) for j in range(pieces)] + [(far, j) for j in halves])
    return orders


def remote(src, dst, send, recv, device):
    return pltpu.make_async_remote_copy(
        src_ref=src, dst_ref=dst, send_sem=send, recv_sem=recv, device_id=device, device_id_type=MESH
    )


def gather_kernel(grid, second, *refs):
    if second:
        x, places, taken = refs[:3]
    else:
        x, home, ids, taken, places = refs[:5]
    held_in, big, members, send, recv, give, take = refs[-7:]
    count, held = held_in.shape[:2]
    groups, group = members.shape[:2]
    width = x.shape[1]
    pieces = held // LANES
    ring = Ring(grid, count)
    orders = hops(ring.chips, pieces)
    where = [{key: t for t, key in enumerate(order)} for order in orders]
    last = len(orders[0])
    ring.greet()

    def part(block, j):
        return held_in.at[block, pl.ds(j * LANES, LANES), :]

    def widen(block, j, source):
        rows = pl.ds(pl.multiple_of(block * held + j * LANES, LANES), LANES)
        big[rows, :] = source[...].astype(jnp.float32)

    started = []

    def start(copy):
        copy.start()
        started.append(copy)

    for j in range(pieces):
        for way in range(2):
            if (1, j) in where[way]:
                t = where[way][(1, j)]
                start(
                    remote(
                        x.at[pl.ds(j * LANES, LANES), :],
                        part(ring.me, j),
                        send.at[way, t],
                        recv.at[way, t],
                        ring.sides[way],
                    )
                )
    start(remote(x, held_in.at[ring.me], give.at[0, last], take.at[0, last], ring.partner))
    for j in range(pieces):
        widen(ring.me, j, x.at[pl.ds(j * LANES, LANES), :])
    other = ring.me + 1 - 2 * ring.core

    def accept(t):
        for way in range(2):
            d, j = orders[way][t]
            block = ring.device(-d if way == 0 else d, 1 - ring.core)
            piece = part(block, j)
            remote(piece, piece, give.at[way, t], take.at[way, t], ring.partner).wait_recv()
            widen(block, j, piece)

    for t in range(last):
        for way in range(2):
            d, j = orders[way][t]
            block = ring.device(-d if way == 0 else d, ring.core)
            piece = part(block, j)
            remote(piece, piece, send.at[way, t], recv.at[way, t], ring.sides[way]).wait_recv()
            onward = where[way].get((d + 1, j))
            if onward is not None:
                start(
                    remote(
                        piece, piece, send.at[way, onward], recv.at[way, onward], ring.sides[way]
                    )
                )
            start(remote(piece, piece, give.at[way, t], take.at[way, t], ring.partner))
            widen(block, j, piece)
        if t == 2:
            remote(
                held_in.at[other], held_in.at[other], give.at[0, last], take.at[0, last], ring.partner
            ).wait_recv()
            for j in range(pieces):
                widen(other, j, part(other, j))
        if t >= LAG:
            accept(t - LAG)
    for t in range(last - LAG, last):
        accept(t)

    def gather_step(r, carry):
        base = r * group
        spots = [places[base + m] if second else home[ids[base + m]] for m in range(group)]
        if not second:
            for m in range(group):
                places[base + m] = spots[m]
        picked = [big[pl.ds(spots[m], 1), :] for m in range(group)]
        for m in range(group):
            members[r, m : m + 1, :] = picked[m]
        return carry

    lax.fori_loop(0, groups, gather_step, 0, unroll=2)

    def narrow_step(b, carry):
        some = LANES // group
        rows = pl.ds(pl.multiple_of(b * LANES, LANES), LANES)
        taken[rows, :] = members[pl.ds(b * some, some)].reshape(LANES, width).astype(taken.dtype)
        return carry

    lax.fori_loop(0, groups * group // LANES, narrow_step, 0)
    for copy in started:
        copy.wait_send()


def gather_rows(x, lists, grid, groups, group):
    count = lax.axis_size("space")
    held, width = x.shape
    entries = groups * group
    last = len(hops(count // 2, held // LANES)[0])
    sems = pltpu.SemaphoreType.DMA
    second = len(lists) == 1
    vmem = pl.BlockSpec(memory_space=pltpu.VMEM)
    smem = pl.BlockSpec(memory_space=pltpu.SMEM)
    outs = [jax.ShapeDtypeStruct((entries, width), x.dtype)]
    out_specs = [vmem]
    if not second:
        outs.append(jax.ShapeDtypeStruct((entries,), jnp.int32))
        out_specs.append(smem)
    return pl.pallas_call(
        functools.partial(gather_kernel, grid, second),
        out_shape=outs,
        in_specs=[vmem] + [smem] * len(lists),
        out_specs=out_specs,
        scratch_shapes=[
            pltpu.VMEM((count, held, width), x.dtype),
            pltpu.VMEM((count * held, width), jnp.float32),
            pltpu.VMEM((groups, group, width), jnp.float32),
            sems((2, last)),
            sems((2, last)),
            sems((2, last + 1)),
            sems((2, last + 1)),
        ],
        compiler_params=pltpu.CompilerParams(
            collective_id=2 if second else 0,
            has_side_effects=True,
            vmem_limit_bytes=60 * 1024 * 1024,
        ),
        name="spread",
    )(x, *lists)


def reduce_kernel(grid, acc, wsum, noisy, out, own, other, got, sent, wother, wgot, wsent, *sems):
    own_sem, give, take, send, recv, wgive, wtake, wsend, wrecv = sems
    chips = acc.shape[0]
    pieces = acc.shape[2] // LANES
    ring = Ring(grid, 2 * chips)
    far = chips // 2
    orders = [
        sorted(order, key=lambda key: (-key[0], key[1])) for order in hops(chips, pieces)
    ]
    where = [{key: t for t, key in enumerate(order)} for order in orders]
    last = len(orders[0])
    offsets = [far] + [s * d for d in range(far - 1, 0, -1) for s in (1, -1)] + [0]
    slot_of = {off: i for i, off in enumerate(offsets)}
    slot_of[-far] = 0
    started, local, gifts = [], [], []

    for i, off in enumerate(offsets):
        copy = pltpu.make_async_copy(acc.at[ring.chip(off), ring.core], own.at[i], own_sem.at[i])
        copy.start()
        local.append(copy)
    ring.greet()
    for i, off in enumerate(offsets):
        copy = remote(
            acc.at[ring.chip(off), 1 - ring.core], other.at[i], give.at[i], take.at[i], ring.partner
        )
        copy.start()
        gifts.append(copy)
        if i == 0:
            wgift = remote(wsum, wother, wgive.at[0], wtake.at[0], ring.partner)
            wgift.start()
    ready = set()

    def settle_slot(i):
        if i not in ready:
            ready.add(i)
            local[i].wait()
            gifts[i].wait_recv()

    def value(off, j, ways, d):
        i = slot_of[off]
        settle_slot(i)
        rows = pl.ds(j * LANES, LANES)
        total = own[i, rows, :].astype(jnp.float32) + other[i, rows, :].astype(jnp.float32)
        for way in ways:
            t = where[way].get((d + 1, j))
            if t is not None:
                piece = got.at[way, t]
                remote(sent.at[way, t], piece, send.at[way, t], recv.at[way, t], ring.sides[way]).wait_recv()
                total = total + piece[...].astype(jnp.float32)
        return total

    def weights(off, ways, d):
        chip = ring.chip(off)
        if "w" not in ready:
            ready.add("w")
            wgift.wait_recv()
        total = wsum[chip, ring.core] + wother[chip, ring.core]
        for way in ways:
            if d + 1 < far or (d + 1 == far and way == 0):
                remote(
                    wsent.at[way, d + 1],
                    wgot.at[way, d + 1],
                    wsend.at[way, d + 1],
                    wrecv.at[way, d + 1],
                    ring.sides[way],
                ).wait_recv()
                total = total + wgot[way, d + 1]
        return total

    for t in range(last):
        for way in range(2):
            d, j = orders[way][t]
            off = d if way == 0 else -d
            sent[way, t] = value(off, j, (way,), d).astype(sent.dtype)
            copy = remote(sent.at[way, t], got.at[way, t], send.at[way, t], recv.at[way, t], ring.sides[way])
            copy.start()
            started.append(copy)
            final_piece = t + 1 == last or orders[way][t + 1][0] != d
            if final_piece and (d < far or way == 0):
                wsent[way, d] = weights(off, (way,), d)
                copy = remote(
                    wsent.at[way, d], wgot.at[way, d], wsend.at[way, d], wrecv.at[way, d], ring.sides[way]
                )
                copy.start()
                started.append(copy)
    lane = lax.broadcasted_iota(jnp.int32, (LANES, LANES), 1)
    sub = lax.broadcasted_iota(jnp.int32, (LANES, LANES), 0)
    denom = weights(0, (0, 1), 0)
    for j in range(pieces):
        rows = pl.ds(j * LANES, LANES)
        numer = value(0, j, (0, 1), 0) + prior_weight * noisy[rows, :].astype(jnp.float32)
        spread = jnp.broadcast_to(denom[j : j + 1, :], (LANES, LANES))
        column = jnp.sum(jnp.where(lane == sub, spread, 0.0), axis=1, keepdims=True)
        out[rows, :] = (numer / (column + prior_weight)).astype(out.dtype)
    for copy in started + gifts + [wgift]:
        copy.wait_send()


def settle(acc, wsum, noisy, grid):
    count = lax.axis_size("space")
    held, width = noisy.shape
    chips, pieces = count // 2, held // LANES
    far = chips // 2
    last = len(hops(chips, pieces)[0])
    sems = pltpu.SemaphoreType.DMA
    vmem = pl.BlockSpec(memory_space=pltpu.VMEM)
    small = (chips, 2, pieces, LANES)
    return pl.pallas_call(
        functools.partial(reduce_kernel, grid),
        out_shape=jax.ShapeDtypeStruct(noisy.shape, noisy.dtype),
        in_specs=[pl.BlockSpec(memory_space=pltpu.HBM), vmem, vmem],
        out_specs=vmem,
        scratch_shapes=[
            pltpu.VMEM((chips, held, width), acc.dtype),
            pltpu.VMEM((chips, held, width), acc.dtype),
            pltpu.VMEM((2, last, LANES, width), acc.dtype),
            pltpu.VMEM((2, last, LANES, width), acc.dtype),
            pltpu.VMEM(small, jnp.float32),
            pltpu.VMEM((2, far + 1, pieces, LANES), jnp.float32),
            pltpu.VMEM((2, far + 1, pieces, LANES), jnp.float32),
            sems((chips,)),
            sems((chips,)),
            sems((chips,)),
            sems((2, last)),
            sems((2, last)),
            sems((1,)),
            sems((1,)),
            sems((2, far + 1)),
            sems((2, far + 1)),
        ],
        compiler_params=pltpu.CompilerParams(
            collective_id=1, has_side_effects=True, vmem_limit_bytes=60 * 1024 * 1024
        ),
        name="settle",
    )(acc.reshape(chips, 2, held, width), wsum.reshape(small), noisy)


def body(grid, noisy, matches, cube_home, sigma_coef):
    groups, group = matches.shape
    cubes = cube_home.shape[0]
    tables = make_tables(group)
    sigma = sigma_coef[None, :]
    members, rows = gather_rows(noisy, (cube_home, matches.reshape(-1)), grid, groups, group)
    coeffs, acc, wsum = phase(False, rows, sigma, tables, members, cubes, group)
    basic = settle(acc, wsum, noisy, grid)
    (guide,) = gather_rows(basic, (rows,), grid, groups, group)
    acc2, wsum2 = phase(True, rows, sigma, tables, guide, cubes, group, coeffs)
    return basic, settle(acc2, wsum2, noisy, grid)


def solution(mesh):
    in_specs = (P(("groups", "space"), None), P(("groups", "space"), None), P("groups"), P())
    out_specs = (P(("groups", "space"), None), P(("groups", "space"), None))
    grid = 2 if mesh.shape["groups"] == 2 else 1
    return jax.shard_map(
        functools.partial(body, grid),
        mesh=mesh,
        in_specs=in_specs,
        out_specs=out_specs,
        check_vma=False,
    )
```
